512 devices in a mesh: scen: 16 (over x, y_hi, core), blk: 32 (over y_lo, z).
Axes of the slice: x: 4, y: 4 (y_hi: 2, y_lo: 2; y = y_hi * 2 + y_lo), z: 16, core: 2. Of those that a mesh axis runs over, the one named last changes fastest.
Arguments:
- blocks: bfloat16 [512, 20, 128, 128], P(('scen', 'blk')), parts along dimension 0, may hold values from -0.125 to 0.125
- col_index: int32 [512, 20], P(('scen', 'blk')), parts along dimension 0, may hold values from 0 to 127, as said below
- cost: float32 [262144], P(('scen', 'blk')), parts along dimension 0, may hold values from -6 to 6
- upper: float32 [262144], P(('scen', 'blk')), parts along dimension 0, may hold values from 0.5 to 1.5
- capacity: float32 [65536], P(('scen', 'blk')), parts along dimension 0, may hold values from 0.5 to 2
- disrupted: int32 [1024, 4096], P('scen', 'blk'), parts along dimension 0, may hold values 0 or 1
- x_start: float32 [1024, 16384], P('scen', 'blk'), parts along dimension 0, may hold values from 0 to 1
- y_start: float32 [1024, 4096], P('scen', 'blk'), parts along dimension 0, may hold values from 0 to 1
Outputs:
- x_final: float32 [1024, 16384], P('scen', 'blk'), parts along dimension 0
- y_final: float32 [1024, 4096], P('scen', 'blk'), parts along dimension 0
The draws below stay inside these ranges and needn't reach their ends.
There are 16 independent parts, one for each index of `scen`. The reference program is written for one: setup_inputs(seed, part) draws one part's arguments, and reference() takes and returns one part's arrays. A program takes and returns all parts, laid end to end along the dimension named above; each array names one. Nothing has to cross between parts.
Inputs may be any that keep to these rules, and one draw needn't show every extreme that they name: `col_index`: with row block r on band device b = r, slot n lies on device (b + n // 4 - 2) modulo the number of devices along the band, that is, its value is that device times 4 plus some column block of it; the first row block of every device takes that device's first column block in slot position 0 and its last in position 1 of each group of 4.
All inputs are finite; a program needn't handle non-finite values. No bound on the sum of `disrupted` on one device may be relied on, other than what follows from the above.
Results may differ from the reference program's by a relative error of at most 0.0025.
Values may be sent and summed in bfloat16 or wider, within the bound.
A program may use at most 64 MiB of HBM per device.

```python
import jax
import jax.numpy as jnp
from jax import lax

RB = 1
CB = 4
BS = 128
REACH = 2
PER_OFF = 4
NB = 20
SCEN = 64
ITERS = 4
NRB = 32
NCB = 128
NROW = 4096
NCOL = 16384
N_BLK = 32


def draw_col_index(key, part):
    rows = jnp.arange(NRB)
    device = rows // RB
    slot = jnp.arange(NB)
    offset = slot // PER_OFF - REACH
    within = jax.random.randint(key, (NRB, NB), 0, CB)
    first = (rows % RB == 0)[:, None]
    position = (slot % PER_OFF)[None, :]
    within = jnp.where(first & (position == 0), 0, within)
    within = jnp.where(first & (position == 1), CB - 1, within)
    owner = (device[:, None] + offset[None, :]) % N_BLK
    return (owner * CB + within).astype(jnp.int32)


def set_ends(entries, key, least, top_value):
    dims = entries.shape
    place = [jax.random.randint(jax.random.fold_in(key, axis), (), 0, dims[axis]) for axis in range(len(dims))]
    entries = entries.at[tuple(place)].set(least)
    longest = dims.index(max(dims))
    place[longest] = (place[longest] + 1) % dims[longest]
    return entries.at[tuple(place)].set(top_value)


def shard_levels(rng, shape, cuts, low, largest):
    gain = 1.0
    for dim, blocks in cuts:
        heights = jax.random.uniform(jax.random.fold_in(jax.random.fold_in(rng, 6), dim), (blocks,), jnp.float32, low / len(cuts), largest / len(cuts))
        gain = gain * jnp.repeat(jnp.exp(heights), shape[dim] // blocks).reshape((-1,) + (1,) * (len(shape) - 1 - dim))
    return gain


def noise(own_key, dims, spread, reach, pieces=(), held_as=jnp.bfloat16):
    array = spread * jax.random.normal(own_key, dims, jnp.float32)
    if pieces:
        array = array * shard_levels(own_key, dims, pieces, -0.22, 0.18)
    return jnp.clip(array, -reach, reach).astype(held_as)


def setup_inputs(seed: int = 0, part: int = 0) -> dict:
    splits = jax.random.split(jax.random.key(seed), 9)
    part_splits = jax.random.split(jax.random.fold_in(splits[8], part), 9)
    blocks = noise(part_splits[0], (NRB, NB, BS, BS), (NB * BS) ** -0.5, 0.125, ((0, 32),))
    col_index = draw_col_index(jax.random.fold_in(jax.random.fold_in(splits[8], part), 71), part)
    cost = noise(part_splits[2], (NCOL,), 1.0, 6.0, ((0, 32),), jnp.float32)
    upper = jnp.clip(0.5 + 1.0 * jax.random.uniform(part_splits[3], (NCOL,), jnp.float32) ** shard_levels(part_splits[3], (NCOL,), ((0, 32),), -0.2, 0.2), 0.5, 1.5)
    capacity = jnp.clip(0.5 + 1.5 * jax.random.uniform(part_splits[4], (NROW,), jnp.float32) ** shard_levels(part_splits[4], (NROW,), ((0, 32),), -0.2, 0.2), 0.5, 2.0)
    disrupted = set_ends((jax.random.randint(part_splits[5], (SCEN, NROW), 0, 8) < 1).astype(jnp.int32), jax.random.fold_in(part_splits[5], 1), 0, 1)
    x_start = jnp.clip(1.0 * jax.random.uniform(part_splits[6], (SCEN, NCOL), jnp.float32) ** shard_levels(part_splits[6], (SCEN, NCOL), ((1, 32),), -0.2, 0.2), 0.0, 1.0)
    y_start = jnp.clip(1.0 * jax.random.uniform(part_splits[7], (SCEN, NROW), jnp.float32) ** shard_levels(part_splits[7], (SCEN, NROW), ((1, 32),), -0.2, 0.2), 0.0, 1.0)
    return dict(blocks=blocks, col_index=col_index, cost=cost, upper=upper, capacity=capacity, disrupted=disrupted, x_start=x_start, y_start=y_start)


step_primal = 0.4
step_dual = 0.4


def apply_k(x_low, blocks, col_index):
    divided_parts = x_low.astype(jnp.float32).reshape(SCEN, NCB, BS)
    selected_entries = jnp.take(divided_parts, col_index.reshape(-1), axis=1).reshape(SCEN, NRB, NB, BS)
    final_output = jnp.einsum("ufol,foql->ufq", selected_entries, blocks.astype(jnp.float32), precision=lax.Precision.HIGHEST)
    return final_output.reshape(SCEN, NROW)


def apply_kt(dual_lower_part, blocks, col_index):
    divided_parts = dual_lower_part.astype(jnp.float32).reshape(SCEN, NRB, BS)
    partial_terms = jnp.einsum("aqd,qudk->quak", divided_parts, blocks.astype(jnp.float32), precision=lax.Precision.HIGHEST)
    summed = jax.ops.segment_sum(partial_terms.reshape(NRB * NB, SCEN, BS), col_index.reshape(-1), num_segments=NCB)
    return jnp.transpose(summed, (1, 0, 2)).reshape(SCEN, NCOL)


def reference(blocks, col_index, cost, upper, capacity, disrupted, x_start, y_start):
    bound = capacity[None, :] * jnp.where(disrupted == 1, 0.25, 1.0)
    primal = x_start
    dual = y_start
    for step in range(ITERS):
        dual_lower_part = dual.astype(jnp.bfloat16)
        pull = cost[None, :] + apply_kt(dual_lower_part, blocks, col_index)
        x_new = jnp.minimum(jnp.maximum(primal - step_primal * pull, 0.0), upper[None, :])
        x_bar = (2.0 * x_new - primal).astype(jnp.bfloat16)
        dual = jnp.maximum(dual + step_dual * (apply_k(x_bar, blocks, col_index) - bound), 0.0)
        primal = x_new
    return primal, dual
```

```python
import functools

import jax
import jax.numpy as jnp
from jax import lax
from jax.experimental import pallas as pl
from jax.experimental.pallas import tpu as pltpu
from jax.sharding import PartitionSpec as P

MESH = pl.DeviceIdType.MESH

REACH = 2
ITERS = 4
SPAN = 2 * REACH + 1
OFFSETS = (-2, 2, -1, 1)

step_primal = 0.4
step_dual = 0.4


def kernel(
    n_dev,
    idx_ref,
    blocks_ref,
    cost_ref,
    upper_ref,
    cap_ref,
    dis_ref,
    xs_ref,
    ys_ref,
    x_out,
    y_out,
    kb,
    head,
    head_in,
    ysend,
    yin,
    zsend,
    zin,
    zown,
    x,
    y,
    cost,
    upper,
    cap,
    dis,
    bound,
    load_sem,
    kb_send,
    kb_recv,
    y_sends,
    y_recvs,
    z_sends,
    z_recvs,
):
    per = kb.shape[1]
    width = kb.shape[2]
    scen = x.shape[0]
    me = lax.axis_index("blk")

    def remote(source, target, send, recv, offset):
        return pltpu.make_async_remote_copy(
            src_ref=source,
            dst_ref=target,
            send_sem=send,
            recv_sem=recv,
            device_id={"blk": lax.rem(me + offset + n_dev, n_dev)},
            device_id_type=MESH,
        )

    loads = [
        pltpu.make_async_copy(ys_ref, y, load_sem.at[0]),
        pltpu.make_async_copy(blocks_ref.at[0, pl.ds(REACH * per, per)], kb.at[REACH], load_sem.at[1]),
        pltpu.make_async_copy(xs_ref, x, load_sem.at[2]),
        pltpu.make_async_copy(cost_ref, cost, load_sem.at[3]),
        pltpu.make_async_copy(upper_ref, upper, load_sem.at[4]),
        pltpu.make_async_copy(cap_ref, cap, load_sem.at[5]),
        pltpu.make_async_copy(dis_ref, dis, load_sem.at[6]),
    ]
    for load in loads:
        load.start()

    barrier = pltpu.get_barrier_semaphore()
    for offset in OFFSETS:
        pl.semaphore_signal(
            barrier, inc=1, device_id={"blk": lax.rem(me + offset + n_dev, n_dev)}, device_id_type=MESH
        )

    head[pl.ds(scen, head.shape[0] - scen), :] = jnp.zeros((head.shape[0] - scen, width), jnp.float32)
    for slot in range(SPAN * per):
        head[pl.ds(scen + slot, 1), :] = jnp.full((1, width), lax.rem(idx_ref[0, slot], per), jnp.float32)
    loads[0].wait()
    head[pl.ds(0, scen), :] = y[...].astype(jnp.bfloat16).astype(jnp.float32)
    ysend[0] = head[...].astype(jnp.bfloat16)

    pl.semaphore_wait(barrier, 2 * REACH)

    heads = {o: remote(ysend.at[0], head_in.at[REACH - o], y_sends.at[0, REACH - o], y_recvs.at[0, REACH - o], o) for o in OFFSETS}
    for o in OFFSETS:
        heads[o].start()
    blocks_out = {
        o: remote(
            blocks_ref.at[0, pl.ds((REACH + o) * per, per)],
            kb.at[REACH - o],
            kb_send.at[REACH - o],
            kb_recv.at[REACH - o],
            o,
        )
        for o in OFFSETS
    }
    for o in (-1, 1, -2, 2):
        blocks_out[o].start()

    for load in loads[1:]:
        load.wait()
    bound[...] = cap[...] * jnp.where(dis[...] == 1, 0.25, 1.0)

    def blocks_of(j):
        return jnp.concatenate([kb[j, s] for s in range(per)], axis=1)

    def marks(j):
        base = scen + (SPAN - 1 - j) * per
        source = head if j == REACH else head_in.at[j]
        rows = source[pl.ds(base, per), :].astype(jnp.float32)
        return [jnp.broadcast_to(rows[s : s + 1, :], (scen, width)) for s in range(per)]

    for it in range(ITERS):
        last = it == ITERS - 1
        acc = [jnp.broadcast_to(cost[:, pl.ds(c * width, width)], (scen, width)) for c in range(per)]
        for j in (2, 1, 3, 0, 4):
            if j == REACH:
                low = ysend[it, pl.ds(0, scen), :]
            else:
                if it == 0:
                    heads[REACH - j].wait_recv()
                    blocks_out[REACH - j].wait_recv()
                    low = head_in[j, pl.ds(0, scen), :]
                else:
                    remote(ysend.at[it, pl.ds(0, scen)], yin.at[it - 1, j], y_sends.at[it, j], y_recvs.at[it, j], REACH - j).wait_recv()
                    low = yin[it - 1, j]
            terms = jnp.dot(low, blocks_of(j), preferred_element_type=jnp.float32)
            acc[0] = acc[0] + terms[:, :width]
            acc[per - 1] = acc[per - 1] + terms[:, width : 2 * width]
            mark = marks(j)
            for s in range(2, per):
                part = terms[:, s * width : (s + 1) * width]
                for c in range(per):
                    acc[c] = acc[c] + jnp.where(mark[s] == c, part, 0.0)
        bars = []
        for c in range(per):
            cols = pl.ds(c * width, width)
            old = x[:, cols]
            new = jnp.minimum(jnp.maximum(old - step_primal * acc[c], 0.0), upper[:, cols])
            bars.append((2.0 * new - old).astype(jnp.bfloat16))
            x[:, cols] = new
        if last:
            x_store = pltpu.make_async_copy(x, x_out, load_sem.at[0])
            x_store.start()
        for j in (0, 4, 1, 3, 2):
            mark = marks(j)
            picked = [bars[0], bars[per - 1]]
            for s in range(2, per):
                chosen = bars[0].astype(jnp.float32)
                for c in range(1, per):
                    chosen = jnp.where(mark[s] == c, bars[c].astype(jnp.float32), chosen)
                picked.append(chosen.astype(jnp.bfloat16))
            terms = lax.dot_general(
                jnp.concatenate(picked, axis=1),
                blocks_of(j),
                (((1,), (1,)), ((), ())),
                preferred_element_type=jnp.float32,
            )
            if j == REACH:
                zown[...] = terms
            else:
                zsend[it, j] = terms
                remote(zsend.at[it, j], zin.at[it, 2 * REACH - j], z_sends.at[it, j], z_recvs.at[it, 2 * REACH - j], j - REACH).start()
        total = zown[...]
        for j in (1, 3, 0, 4):
            remote(zsend.at[it, j], zin.at[it, j], z_sends.at[it, j], z_recvs.at[it, j], REACH - j).wait_recv()
            total = total + zin[it, j]
        new_y = jnp.maximum(y[...] + step_dual * (total - bound[...]), 0.0)
        y[...] = new_y
        if not last:
            ysend[it + 1, pl.ds(0, scen), :] = new_y.astype(jnp.bfloat16)
            for o in OFFSETS:
                remote(
                    ysend.at[it + 1, pl.ds(0, scen)],
                    yin.at[it, REACH - o],
                    y_sends.at[it + 1, REACH - o],
                    y_recvs.at[it + 1, REACH - o],
                    o,
                ).start()
    y_store = pltpu.make_async_copy(y, y_out, load_sem.at[1])
    y_store.start()
    for o in OFFSETS:
        heads[o].wait_send()
        blocks_out[o].wait_send()
        for it in range(1, ITERS):
            remote(ysend.at[it, pl.ds(0, scen)], yin.at[it - 1, REACH - o], y_sends.at[it, REACH - o], y_recvs.at[it, REACH - o], o).wait_send()
        for it in range(ITERS):
            j = o + REACH
            remote(zsend.at[it, j], zin.at[it, j], z_sends.at[it, j], z_recvs.at[it, j], o).wait_send()
    x_store.wait()
    y_store.wait()


def per_device(n_dev, blocks, col_index, cost, upper, capacity, disrupted, x_start, y_start):
    slots, width = blocks.shape[1], blocks.shape[3]
    per = slots // SPAN
    scen, ncols = x_start.shape
    rows_head = scen + 32
    f32, bf16 = jnp.float32, jnp.bfloat16
    anyspace = pl.BlockSpec(memory_space=pl.ANY)
    dma = pltpu.SemaphoreType.DMA
    return pl.pallas_call(
        functools.partial(kernel, n_dev),
        out_shape=(
            jax.ShapeDtypeStruct(x_start.shape, f32),
            jax.ShapeDtypeStruct(y_start.shape, f32),
        ),
        in_specs=[pl.BlockSpec(memory_space=pltpu.SMEM)] + [anyspace] * 7,
        out_specs=(anyspace, anyspace),
        scratch_shapes=[
            pltpu.VMEM((SPAN, per, width, width), bf16),
            pltpu.VMEM((rows_head, width), f32),
            pltpu.VMEM((SPAN, rows_head, width), bf16),
            pltpu.VMEM((ITERS, rows_head, width), bf16),
            pltpu.VMEM((ITERS - 1, SPAN, scen, width), bf16),
            pltpu.VMEM((ITERS, SPAN, scen, width), f32),
            pltpu.VMEM((ITERS, SPAN, scen, width), f32),
            pltpu.VMEM((scen, width), f32),
            pltpu.VMEM((scen, ncols), f32),
            pltpu.VMEM((scen, width), f32),
            pltpu.VMEM((1, ncols), f32),
            pltpu.VMEM((1, ncols), f32),
            pltpu.VMEM((1, width), f32),
            pltpu.VMEM((scen, width), jnp.int32),
            pltpu.VMEM((scen, width), f32),
            dma((7,)),
            dma((SPAN,)),
            dma((SPAN,)),
            dma((ITERS, SPAN)),
            dma((ITERS, SPAN)),
            dma((ITERS, SPAN)),
            dma((ITERS, SPAN)),
        ],
        compiler_params=pltpu.CompilerParams(
            collective_id=0, has_side_effects=True, vmem_limit_bytes=32 * 1024 * 1024
        ),
    )(
        col_index,
        blocks,
        cost.reshape(1, -1),
        upper.reshape(1, -1),
        capacity.reshape(1, -1),
        disrupted,
        x_start,
        y_start,
    )


def solution(mesh):
    placed = (
        P(("scen", "blk"), None, None, None),
        P(("scen", "blk"), None),
        P(("scen", "blk")),
        P(("scen", "blk")),
        P(("scen", "blk")),
        P("scen", "blk"),
        P("scen", "blk"),
        P("scen", "blk"),
    )
    return jax.shard_map(
        functools.partial(per_device, mesh.shape["blk"]),
        mesh=mesh,
        in_specs=placed,
        out_specs=(P("scen", "blk"), P("scen", "blk")),
        check_vma=False,
    )
```

```python
import functools

import jax
import jax.numpy as jnp
from jax import lax
from jax.experimental import pallas as pl
from jax.experimental.pallas import tpu as pltpu
from jax.sharding import PartitionSpec as P

MESH = pl.DeviceIdType.MESH

REACH = 2
ITERS = 4
SPAN = 2 * REACH + 1
OFFSETS = (-2, 2, -1, 1)

step_primal = 0.4
step_dual = 0.4


def kernel(
    n_dev,
    paired,
    idx_hbm,
    blocks_ref,
    cost_ref,
    upper_ref,
    cap_ref,
    dis_ref,
    xs_ref,
    ys_ref,
    x_out,
    y_out,
    idx_ref,
    kb,
    head,
    head_in,
    ysend,
    yin,
    zsend,
    zin,
    zown,
    zheld,
    zsum,
    x,
    y,
    cost,
    upper,
    cap,
    dis,
    bound,
    load_sem,
    kb_send,
    kb_recv,
    y_sends,
    y_recvs,
    z_sends,
    z_recvs,
    turn,
):
    per = kb.shape[1]
    width = kb.shape[2]
    scen = x.shape[0]
    me = lax.axis_index("blk")

    def remote(source, target, send, recv, offset):
        return pltpu.make_async_remote_copy(
            src_ref=source,
            dst_ref=target,
            send_sem=send,
            recv_sem=recv,
            device_id={"blk": lax.rem(me + offset + n_dev, n_dev)},
            device_id_type=MESH,
        )

    barrier = pltpu.get_barrier_semaphore()
    for offset in OFFSETS:
        pl.semaphore_signal(
            barrier, inc=1, device_id={"blk": lax.rem(me + offset + n_dev, n_dev)}, device_id_type=MESH
        )
    if paired:
        group = lax.axis_index("scen")
        second = lax.rem(group, 2)
        twin = {"scen": group + 1 - 2 * second}
        pl.semaphore_signal(barrier, inc=1, device_id=twin, device_id_type=MESH)

    loads = [
        pltpu.make_async_copy(ys_ref, y, load_sem.at[0]),
        pltpu.make_async_copy(idx_hbm, idx_ref, load_sem.at[7]),
        pltpu.make_async_copy(blocks_ref.at[0, pl.ds(REACH * per, per)], kb.at[REACH], load_sem.at[1]),
        pltpu.make_async_copy(xs_ref, x, load_sem.at[2]),
        pltpu.make_async_copy(cost_ref, cost, load_sem.at[3]),
        pltpu.make_async_copy(upper_ref, upper, load_sem.at[4]),
        pltpu.make_async_copy(cap_ref, cap, load_sem.at[5]),
        pltpu.make_async_copy(dis_ref, dis, load_sem.at[6]),
    ]
    for load in loads:
        load.start()
    blocks_out = {
        o: remote(
            blocks_ref.at[0, pl.ds((REACH + o) * per, per)],
            kb.at[REACH - o],
            kb_send.at[REACH - o],
            kb_recv.at[REACH - o],
            o,
        )
        for o in OFFSETS
    }

    def send_blocks(offsets):
        for o in offsets:
            blocks_out[o].start()

    pl.semaphore_wait(barrier, 2 * REACH + (1 if paired else 0))
    if paired:
        pl.when(second == 0)(lambda: send_blocks((-1, 1)))
    else:
        send_blocks((-1, 1))

    loads[0].wait()
    loads[1].wait()
    head[pl.ds(scen, head.shape[0] - scen), :] = jnp.zeros((head.shape[0] - scen, width), jnp.float32)
    for slot in range(SPAN * per):
        head[pl.ds(scen + slot, 1), :] = jnp.full((1, width), lax.rem(idx_ref[0, slot], per), jnp.float32)
    head[pl.ds(0, scen), :] = y[...].astype(jnp.bfloat16).astype(jnp.float32)
    ysend[0] = head[...].astype(jnp.bfloat16)
    heads = {o: remote(ysend.at[0], head_in.at[REACH - o], y_sends.at[0, REACH - o], y_recvs.at[0, REACH - o], o) for o in OFFSETS}
    for o in OFFSETS:
        heads[o].start()
    if paired:
        pl.when(second == 0)(lambda: send_blocks((-2, 2)))

        @pl.when(second == 1)
        def _():
            pl.semaphore_wait(turn, 1)
            send_blocks((-1, 1, -2, 2))
    else:
        send_blocks((-2, 2))

    for load in loads[2:]:
        load.wait()
    bound[...] = cap[...] * jnp.where(dis[...] == 1, 0.25, 1.0)

    def blocks_of(j):
        return jnp.concatenate([kb[j, s] for s in range(per)], axis=1)

    def marks(j):
        base = scen + (SPAN - 1 - j) * per
        source = head if j == REACH else head_in.at[j]
        rows = source[pl.ds(base, per), :].astype(jnp.float32)
        return [jnp.broadcast_to(rows[s : s + 1, :], (scen, width)) for s in range(per)]

    for it in range(ITERS):
        last = it == ITERS - 1
        acc = [jnp.broadcast_to(cost[:, pl.ds(c * width, width)], (scen, width)) for c in range(per)]
        for j in (REACH, 1, 3, 0, 4):
            if j == REACH:
                low = ysend[it, pl.ds(0, scen), :]
            else:
                if it == 0:
                    heads[REACH - j].wait_recv()
                    blocks_out[REACH - j].wait_recv()
                    if paired and j == REACH + 1:

                        @pl.when(second == 0)
                        def _():
                            pl.semaphore_signal(turn, inc=1, device_id=twin, device_id_type=MESH)
                    low = head_in[j, pl.ds(0, scen), :]
                else:
                    remote(ysend.at[it, pl.ds(0, scen)], yin.at[it - 1, j], y_sends.at[it, j], y_recvs.at[it, j], REACH - j).wait_recv()
                    low = yin[it - 1, j]
            terms = jnp.dot(low, blocks_of(j), preferred_element_type=jnp.float32)
            acc[0] = acc[0] + terms[:, :width]
            acc[per - 1] = acc[per - 1] + terms[:, width : 2 * width]
            mark = marks(j)
            for s in range(2, per):
                part = terms[:, s * width : (s + 1) * width]
                for c in range(per):
                    acc[c] = acc[c] + jnp.where(mark[s] == c, part, 0.0)
        bars = []
        for c in range(per):
            cols = pl.ds(c * width, width)
            old = x[:, cols]
            new = jnp.minimum(jnp.maximum(old - step_primal * acc[c], 0.0), upper[:, cols])
            bars.append((2.0 * new - old).astype(jnp.bfloat16))
            x[:, cols] = new
        if last:
            x_store = pltpu.make_async_copy(x, x_out, load_sem.at[0])
            x_store.start()
        for j in (0, 4, 1, 3, 2):
            mark = marks(j)
            picked = [bars[0], bars[per - 1]]
            for s in range(2, per):
                chosen = bars[0].astype(jnp.float32)
                for c in range(1, per):
                    chosen = jnp.where(mark[s] == c, bars[c].astype(jnp.float32), chosen)
                picked.append(chosen.astype(jnp.bfloat16))
            terms = lax.dot_general(
                jnp.concatenate(picked, axis=1),
                blocks_of(j),
                (((1,), (1,)), ((), ())),
                preferred_element_type=jnp.float32,
            )
            if j == REACH:
                zown[...] = terms
            else:
                change = (terms if it == 0 else terms - zheld[j]).astype(jnp.bfloat16)
                zsend[it, j] = change
                if not last:
                    zheld[j] = change.astype(jnp.float32) if it == 0 else zheld[j] + change.astype(jnp.float32)
                remote(zsend.at[it, j], zin.at[it, 2 * REACH - j], z_sends.at[it, j], z_recvs.at[it, 2 * REACH - j], j - REACH).start()
        others = jnp.zeros((scen, width), jnp.float32) if it == 0 else zsum[...]
        for j in (1, 3, 0, 4):
            remote(zsend.at[it, j], zin.at[it, j], z_sends.at[it, j], z_recvs.at[it, j], REACH - j).wait_recv()
            others = others + zin[it, j].astype(jnp.float32)
        if not last:
            zsum[...] = others
        new_y = jnp.maximum(y[...] + step_dual * (zown[...] + others - bound[...]), 0.0)
        y[...] = new_y
        if not last:
            ysend[it + 1, pl.ds(0, scen), :] = new_y.astype(jnp.bfloat16)
            for o in OFFSETS:
                remote(
                    ysend.at[it + 1, pl.ds(0, scen)],
                    yin.at[it, REACH - o],
                    y_sends.at[it + 1, REACH - o],
                    y_recvs.at[it + 1, REACH - o],
                    o,
                ).start()
    y_store = pltpu.make_async_copy(y, y_out, load_sem.at[1])
    y_store.start()
    for o in OFFSETS:
        heads[o].wait_send()
        blocks_out[o].wait_send()
        for it in range(1, ITERS):
            remote(ysend.at[it, pl.ds(0, scen)], yin.at[it - 1, REACH - o], y_sends.at[it, REACH - o], y_recvs.at[it, REACH - o], o).wait_send()
        for it in range(ITERS):
            j = o + REACH
            remote(zsend.at[it, j], zin.at[it, j], z_sends.at[it, j], z_recvs.at[it, j], o).wait_send()
    x_store.wait()
    y_store.wait()


def finish(x_in, y_in, x_out, y_out, sems):
    copies = [
        pltpu.make_async_copy(x_in, x_out, sems.at[0]),
        pltpu.make_async_copy(y_in, y_out, sems.at[1]),
    ]
    for copy in copies:
        copy.start()
    for copy in copies:
        copy.wait()


def per_device(n_dev, paired, blocks, col_index, cost, upper, capacity, disrupted, x_start, y_start):
    slots, width = blocks.shape[1], blocks.shape[3]
    per = slots // SPAN
    scen, ncols = x_start.shape
    rows_head = scen + 32
    f32, bf16 = jnp.float32, jnp.bfloat16
    anyspace = pl.BlockSpec(memory_space=pl.ANY)
    dma = pltpu.SemaphoreType.DMA
    shapes = (
        jax.ShapeDtypeStruct(x_start.shape, f32),
        jax.ShapeDtypeStruct(y_start.shape, f32),
    )
    ends = pl.pallas_call(
        functools.partial(kernel, n_dev, paired),
        out_shape=shapes,
        in_specs=[anyspace] * 8,
        out_specs=(anyspace, anyspace),
        scratch_shapes=[
            pltpu.SMEM(col_index.shape, jnp.int32),
            pltpu.VMEM((SPAN, per, width, width), bf16),
            pltpu.VMEM((rows_head, width), f32),
            pltpu.VMEM((SPAN, rows_head, width), bf16),
            pltpu.VMEM((ITERS, rows_head, width), bf16),
            pltpu.VMEM((ITERS - 1, SPAN, scen, width), bf16),
            pltpu.VMEM((ITERS, SPAN, scen, width), bf16),
            pltpu.VMEM((ITERS, SPAN, scen, width), bf16),
            pltpu.VMEM((scen, width), f32),
            pltpu.VMEM((SPAN, scen, width), f32),
            pltpu.VMEM((scen, width), f32),
            pltpu.VMEM((scen, ncols), f32),
            pltpu.VMEM((scen, width), f32),
            pltpu.VMEM((1, ncols), f32),
            pltpu.VMEM((1, ncols), f32),
            pltpu.VMEM((1, width), f32),
            pltpu.VMEM((scen, width), jnp.int32),
            pltpu.VMEM((scen, width), f32),
            dma((8,)),
            dma((SPAN,)),
            dma((SPAN,)),
            dma((ITERS, SPAN)),
            dma((ITERS, SPAN)),
            dma((ITERS, SPAN)),
            dma((ITERS, SPAN)),
            pltpu.SemaphoreType.REGULAR,
        ],
        compiler_params=pltpu.CompilerParams(
            collective_id=0, has_side_effects=True, vmem_limit_bytes=60 * 1024 * 1024
        ),
    )(
        col_index,
        blocks,
        cost.reshape(1, -1),
        upper.reshape(1, -1),
        capacity.reshape(1, -1),
        disrupted,
        x_start,
        y_start,
    )
    return pl.pallas_call(
        finish,
        out_shape=shapes,
        in_specs=[anyspace] * 2,
        out_specs=(anyspace, anyspace),
        scratch_shapes=[dma((2,))],
    )(*ends)


def solution(mesh):
    placed = (
        P(("scen", "blk"), None, None, None),
        P(("scen", "blk"), None),
        P(("scen", "blk")),
        P(("scen", "blk")),
        P(("scen", "blk")),
        P("scen", "blk"),
        P("scen", "blk"),
        P("scen", "blk"),
    )
    return jax.shard_map(
        functools.partial(per_device, mesh.shape["blk"], mesh.shape["scen"] % 2 == 0),
        mesh=mesh,
        in_specs=placed,
        out_specs=(P("scen", "blk"), P("scen", "blk")),
        check_vma=False,
    )
```

```python
import functools

import jax
import jax.numpy as jnp
from jax import lax
from jax.experimental import pallas as pl
from jax.experimental.pallas import tpu as pltpu
from jax.sharding import PartitionSpec as P

MESH = pl.DeviceIdType.MESH

REACH = 2
ITERS = 4
SPAN = 2 * REACH + 1
OFFSETS = (-2, 2, -1, 1)

step_primal = 0.4
step_dual = 0.4


def kernel(
    n_dev,
    paired,
    idx_hbm,
    blocks_ref,
    cost_ref,
    upper_ref,
    cap_ref,
    dis_ref,
    xs_ref,
    ys_ref,
    x,
    y,
    idx_ref,
    kb,
    head,
    head_in,
    ysend,
    yin,
    zsend,
    zin,
    zown,
    zheld,
    zsum,
    cost,
    upper,
    cap,
    dis,
    bound,
    load_sem,
    kb_send,
    kb_recv,
    y_sends,
    y_recvs,
    z_sends,
    z_recvs,
    turn,
):
    per = kb.shape[1]
    width = kb.shape[2]
    scen = x.shape[0]
    me = lax.axis_index("blk")

    def remote(source, target, send, recv, offset):
        return pltpu.make_async_remote_copy(
            src_ref=source,
            dst_ref=target,
            send_sem=send,
            recv_sem=recv,
            device_id={"blk": lax.rem(me + offset + n_dev, n_dev)},
            device_id_type=MESH,
        )

    barrier = pltpu.get_barrier_semaphore()
    for offset in OFFSETS:
        pl.semaphore_signal(
            barrier, inc=1, device_id={"blk": lax.rem(me + offset + n_dev, n_dev)}, device_id_type=MESH
        )
    if paired:
        group = lax.axis_index("scen")
        second = lax.rem(group, 2)
        twin = {"scen": group + 1 - 2 * second}
        pl.semaphore_signal(barrier, inc=1, device_id=twin, device_id_type=MESH)

    loads = [
        pltpu.make_async_copy(ys_ref, y, load_sem.at[0]),
        pltpu.make_async_copy(idx_hbm, idx_ref, load_sem.at[7]),
        pltpu.make_async_copy(blocks_ref.at[0, pl.ds(REACH * per, per)], kb.at[REACH], load_sem.at[1]),
        pltpu.make_async_copy(xs_ref, x, load_sem.at[2]),
        pltpu.make_async_copy(cost_ref, cost, load_sem.at[3]),
        pltpu.make_async_copy(upper_ref, upper, load_sem.at[4]),
        pltpu.make_async_copy(cap_ref, cap, load_sem.at[5]),
        pltpu.make_async_copy(dis_ref, dis, load_sem.at[6]),
    ]
    for load in loads:
        load.start()
    blocks_out = {
        o: remote(
            blocks_ref.at[0, pl.ds((REACH + o) * per, per)],
            kb.at[REACH - o],
            kb_send.at[REACH - o],
            kb_recv.at[REACH - o],
            o,
        )
        for o in OFFSETS
    }

    def send_blocks(offsets):
        for o in offsets:
            blocks_out[o].start()

    pl.semaphore_wait(barrier, 2 * REACH + (1 if paired else 0))
    if paired:
        pl.when(second == 0)(lambda: send_blocks((-1, 1)))
    else:
        send_blocks((-1, 1))

    loads[0].wait()
    loads[1].wait()
    head[pl.ds(scen, head.shape[0] - scen), :] = jnp.zeros((head.shape[0] - scen, width), jnp.float32)
    for slot in range(SPAN * per):
        head[pl.ds(scen + slot, 1), :] = jnp.full((1, width), lax.rem(idx_ref[0, slot], per), jnp.float32)
    head[pl.ds(0, scen), :] = y[...].astype(jnp.bfloat16).astype(jnp.float32)
    ysend[0] = head[...].astype(jnp.bfloat16)
    heads = {o: remote(ysend.at[0], head_in.at[REACH - o], y_sends.at[0, REACH - o], y_recvs.at[0, REACH - o], o) for o in OFFSETS}
    for o in OFFSETS:
        heads[o].start()
    if paired:
        pl.when(second == 0)(lambda: send_blocks((-2, 2)))

        @pl.when(second == 1)
        def _():
            pl.semaphore_wait(turn, 1)
            send_blocks((-1, 1, -2, 2))
    else:
        send_blocks((-2, 2))

    for load in loads[2:]:
        load.wait()
    bound[...] = cap[...] * jnp.where(dis[...] == 1, 0.25, 1.0)

    def blocks_of(j):
        return jnp.concatenate([kb[j, s] for s in range(per)], axis=1)

    def marks(j):
        base = scen + (SPAN - 1 - j) * per
        source = head if j == REACH else head_in.at[j]
        rows = source[pl.ds(base, per), :].astype(jnp.float32)
        return [jnp.broadcast_to(rows[s : s + 1, :], (scen, width)) for s in range(per)]

    for it in range(ITERS):
        last = it == ITERS - 1
        acc = [jnp.broadcast_to(cost[:, pl.ds(c * width, width)], (scen, width)) for c in range(per)]
        for j in (REACH, 1, 3, 0, 4):
            if j == REACH:
                low = ysend[it, pl.ds(0, scen), :]
            else:
                if it == 0:
                    heads[REACH - j].wait_recv()
                    blocks_out[REACH - j].wait_recv()
                    if paired and j == REACH + 1:

                        @pl.when(second == 0)
                        def _():
                            pl.semaphore_signal(turn, inc=1, device_id=twin, device_id_type=MESH)
                    low = head_in[j, pl.ds(0, scen), :]
                else:
                    remote(ysend.at[it, pl.ds(0, scen)], yin.at[it - 1, j], y_sends.at[it, j], y_recvs.at[it, j], REACH - j).wait_recv()
                    low = yin[it - 1, j]
            terms = jnp.dot(low, blocks_of(j), preferred_element_type=jnp.float32)
            acc[0] = acc[0] + terms[:, :width]
            acc[per - 1] = acc[per - 1] + terms[:, width : 2 * width]
            mark = marks(j)
            for s in range(2, per):
                part = terms[:, s * width : (s + 1) * width]
                for c in range(per):
                    acc[c] = acc[c] + jnp.where(mark[s] == c, part, 0.0)
        bars = []
        for c in range(per):
            cols = pl.ds(c * width, width)
            old = x[:, cols]
            new = jnp.minimum(jnp.maximum(old - step_primal * acc[c], 0.0), upper[:, cols])
            bars.append((2.0 * new - old).astype(jnp.bfloat16))
            x[:, cols] = new
        for j in (0, 4, 1, 3, 2):
            mark = marks(j)
            picked = [bars[0], bars[per - 1]]
            for s in range(2, per):
                chosen = bars[0].astype(jnp.float32)
                for c in range(1, per):
                    chosen = jnp.where(mark[s] == c, bars[c].astype(jnp.float32), chosen)
                picked.append(chosen.astype(jnp.bfloat16))
            terms = lax.dot_general(
                jnp.concatenate(picked, axis=1),
                blocks_of(j),
                (((1,), (1,)), ((), ())),
                preferred_element_type=jnp.float32,
            )
            if j == REACH:
                zown[...] = terms
            else:
                change = (terms if it == 0 else terms - zheld[j]).astype(jnp.bfloat16)
                zsend[it, j] = change
                if not last:
                    zheld[j] = change.astype(jnp.float32) if it == 0 else zheld[j] + change.astype(jnp.float32)
                remote(zsend.at[it, j], zin.at[it, 2 * REACH - j], z_sends.at[it, j], z_recvs.at[it, 2 * REACH - j], j - REACH).start()
        others = jnp.zeros((scen, width), jnp.float32) if it == 0 else zsum[...]
        for j in (1, 3, 0, 4):
            remote(zsend.at[it, j], zin.at[it, j], z_sends.at[it, j], z_recvs.at[it, j], REACH - j).wait_recv()
            others = others + zin[it, j].astype(jnp.float32)
        if not last:
            zsum[...] = others
        new_y = jnp.maximum(y[...] + step_dual * (zown[...] + others - bound[...]), 0.0)
        y[...] = new_y
        if not last:
            ysend[it + 1, pl.ds(0, scen), :] = new_y.astype(jnp.bfloat16)
            for o in OFFSETS:
                remote(
                    ysend.at[it + 1, pl.ds(0, scen)],
                    yin.at[it, REACH - o],
                    y_sends.at[it + 1, REACH - o],
                    y_recvs.at[it + 1, REACH - o],
                    o,
                ).start()
    for o in OFFSETS:
        heads[o].wait_send()
        blocks_out[o].wait_send()
        for it in range(1, ITERS):
            remote(ysend.at[it, pl.ds(0, scen)], yin.at[it - 1, REACH - o], y_sends.at[it, REACH - o], y_recvs.at[it, REACH - o], o).wait_send()
        for it in range(ITERS):
            j = o + REACH
            remote(zsend.at[it, j], zin.at[it, j], z_sends.at[it, j], z_recvs.at[it, j], o).wait_send()


def per_device(n_dev, paired, blocks, col_index, cost, upper, capacity, disrupted, x_start, y_start):
    slots, width = blocks.shape[1], blocks.shape[3]
    per = slots // SPAN
    scen, ncols = x_start.shape
    rows_head = scen + 32
    f32, bf16 = jnp.float32, jnp.bfloat16
    anyspace = pl.BlockSpec(memory_space=pl.ANY)
    dma = pltpu.SemaphoreType.DMA
    shapes = (
        jax.ShapeDtypeStruct(x_start.shape, f32),
        jax.ShapeDtypeStruct(y_start.shape, f32),
    )
    ends = pl.pallas_call(
        functools.partial(kernel, n_dev, paired),
        out_shape=shapes,
        in_specs=[anyspace] * 8,
        out_specs=(pl.BlockSpec(memory_space=pltpu.VMEM),) * 2,
        scratch_shapes=[
            pltpu.SMEM(col_index.shape, jnp.int32),
            pltpu.VMEM((SPAN, per, width, width), bf16),
            pltpu.VMEM((rows_head, width), f32),
            pltpu.VMEM((SPAN, rows_head, width), bf16),
            pltpu.VMEM((ITERS, rows_head, width), bf16),
            pltpu.VMEM((ITERS - 1, SPAN, scen, width), bf16),
            pltpu.VMEM((ITERS, SPAN, scen, width), bf16),
            pltpu.VMEM((ITERS, SPAN, scen, width), bf16),
            pltpu.VMEM((scen, width), f32),
            pltpu.VMEM((SPAN, scen, width), f32),
            pltpu.VMEM((scen, width), f32),
            pltpu.VMEM((1, ncols), f32),
            pltpu.VMEM((1, ncols), f32),
            pltpu.VMEM((1, width), f32),
            pltpu.VMEM((scen, width), jnp.int32),
            pltpu.VMEM((scen, width), f32),
            dma((8,)),
            dma((SPAN,)),
            dma((SPAN,)),
            dma((ITERS, SPAN)),
            dma((ITERS, SPAN)),
            dma((ITERS, SPAN)),
            dma((ITERS, SPAN)),
            pltpu.SemaphoreType.REGULAR,
        ],
        compiler_params=pltpu.CompilerParams(
            collective_id=0, has_side_effects=True, vmem_limit_bytes=32 * 1024 * 1024
        ),
    )(
        *(
            pltpu.with_memory_space_constraint(operand, pltpu.HBM)
            for operand in (
                col_index,
                blocks,
                cost.reshape(1, -1),
                upper.reshape(1, -1),
                capacity.reshape(1, -1),
                disrupted,
                x_start,
                y_start,
            )
        )
    )
    return ends


def solution(mesh):
    placed = (
        P(("scen", "blk"), None, None, None),
        P(("scen", "blk"), None),
        P(("scen", "blk")),
        P(("scen", "blk")),
        P(("scen", "blk")),
        P("scen", "blk"),
        P("scen", "blk"),
        P("scen", "blk"),
    )
    return jax.shard_map(
        functools.partial(per_device, mesh.shape["blk"], mesh.shape["scen"] % 2 == 0),
        mesh=mesh,
        in_specs=placed,
        out_specs=(P("scen", "blk"), P("scen", "blk")),
        check_vma=False,
    )
```

```python
import functools

import jax
import jax.numpy as jnp
from jax import lax
from jax.experimental import pallas as pl
from jax.experimental.pallas import tpu as pltpu
from jax.sharding import PartitionSpec as P

MESH = pl.DeviceIdType.MESH

REACH = 2
ITERS = 4
SPAN = 2 * REACH + 1
OFFSETS = (-2, 2, -1, 1)

step_primal = 0.4
step_dual = 0.4


def kernel(
    n_dev,
    paired,
    idx_hbm,
    blocks_ref,
    cost_ref,
    upper_ref,
    cap_ref,
    dis_ref,
    xs_ref,
    ys_ref,
    x,
    y,
    idx_ref,
    kb,
    kt,
    head,
    head_in,
    ysend,
    yin,
    zsend,
    zin,
    zown,
    zheld,
    zsum,
    cost,
    upper,
    cap,
    dis,
    bound,
    load_sem,
    kb_send,
    kb_recv,
    y_sends,
    y_recvs,
    z_sends,
    z_recvs,
    turn,
):
    per = kb.shape[1]
    width = kb.shape[2]
    scen = x.shape[0]
    me = lax.axis_index("blk")

    def remote(source, target, send, recv, offset):
        return pltpu.make_async_remote_copy(
            src_ref=source,
            dst_ref=target,
            send_sem=send,
            recv_sem=recv,
            device_id={"blk": lax.rem(me + offset + n_dev, n_dev)},
            device_id_type=MESH,
        )

    barrier = pltpu.get_barrier_semaphore()
    for offset in OFFSETS:
        pl.semaphore_signal(
            barrier, inc=1, device_id={"blk": lax.rem(me + offset + n_dev, n_dev)}, device_id_type=MESH
        )
    if paired:
        group = lax.axis_index("scen")
        second = lax.rem(group, 2)
        twin = {"scen": group + 1 - 2 * second}
        pl.semaphore_signal(barrier, inc=1, device_id=twin, device_id_type=MESH)

    loads = [
        pltpu.make_async_copy(ys_ref, y, load_sem.at[0]),
        pltpu.make_async_copy(idx_hbm, idx_ref, load_sem.at[7]),
        pltpu.make_async_copy(blocks_ref.at[0, pl.ds(REACH * per, per)], kb.at[REACH], load_sem.at[1]),
        pltpu.make_async_copy(xs_ref, x, load_sem.at[2]),
        pltpu.make_async_copy(cost_ref, cost, load_sem.at[3]),
        pltpu.make_async_copy(upper_ref, upper, load_sem.at[4]),
        pltpu.make_async_copy(cap_ref, cap, load_sem.at[5]),
        pltpu.make_async_copy(dis_ref, dis, load_sem.at[6]),
    ]
    for load in loads:
        load.start()
    blocks_out = {
        o: remote(
            blocks_ref.at[0, pl.ds((REACH + o) * per, per)],
            kb.at[REACH - o],
            kb_send.at[REACH - o],
            kb_recv.at[REACH - o],
            o,
        )
        for o in OFFSETS
    }

    def send_blocks(offsets):
        for o in offsets:
            blocks_out[o].start()

    pl.semaphore_wait(barrier, 2 * REACH + (1 if paired else 0))
    if paired:
        pl.when(second == 0)(lambda: send_blocks((-1, 1)))
    else:
        send_blocks((-1, 1))

    loads[0].wait()
    loads[1].wait()
    head[pl.ds(scen, head.shape[0] - scen), :] = jnp.zeros((head.shape[0] - scen, width), jnp.float32)
    for slot in range(SPAN * per):
        head[pl.ds(scen + slot, 1), :] = jnp.full((1, width), lax.rem(idx_ref[0, slot], per), jnp.float32)
    head[pl.ds(0, scen), :] = y[...].astype(jnp.bfloat16).astype(jnp.float32)
    ysend[0] = head[...].astype(jnp.bfloat16)
    heads = {o: remote(ysend.at[0], head_in.at[REACH - o], y_sends.at[0, REACH - o], y_recvs.at[0, REACH - o], o) for o in OFFSETS}
    for o in OFFSETS:
        heads[o].start()
    if paired:
        pl.when(second == 0)(lambda: send_blocks((-2, 2)))

        @pl.when(second == 1)
        def _():
            pl.semaphore_wait(turn, 1)
            send_blocks((-1, 1, -2, 2))
    else:
        send_blocks((-2, 2))

    for load in loads[2:]:
        load.wait()
    bound[...] = cap[...] * jnp.where(dis[...] == 1, 0.25, 1.0)

    def blocks_of(j):
        return jnp.concatenate([kb[j, s] for s in range(per)], axis=1)

    def marks(j):
        base = scen + (SPAN - 1 - j) * per
        source = head if j == REACH else head_in.at[j]
        rows = source[pl.ds(base, per), :].astype(jnp.float32)
        return [jnp.broadcast_to(rows[s : s + 1, :], (scen, width)) for s in range(per)]

    for it in range(ITERS):
        last = it == ITERS - 1
        acc = [jnp.broadcast_to(cost[:, pl.ds(c * width, width)], (scen, width)) for c in range(per)]
        for j in (REACH, 1, 3, 0, 4):
            if j == REACH:
                low = ysend[it, pl.ds(0, scen), :]
            else:
                if it == 0:
                    heads[REACH - j].wait_recv()
                    blocks_out[REACH - j].wait_recv()
                    if paired and j == REACH + 1:

                        @pl.when(second == 0)
                        def _():
                            pl.semaphore_signal(turn, inc=1, device_id=twin, device_id_type=MESH)
                    low = head_in[j, pl.ds(0, scen), :]
                else:
                    remote(ysend.at[it, pl.ds(0, scen)], yin.at[it - 1, j], y_sends.at[it, j], y_recvs.at[it, j], REACH - j).wait_recv()
                    low = yin[it - 1, j]
            terms = jnp.dot(low, blocks_of(j), preferred_element_type=jnp.float32)
            acc[0] = acc[0] + terms[:, :width]
            acc[per - 1] = acc[per - 1] + terms[:, width : 2 * width]
            mark = marks(j)
            for s in range(2, per):
                part = terms[:, s * width : (s + 1) * width]
                for c in range(per):
                    acc[c] = acc[c] + jnp.where(mark[s] == c, part, 0.0)
        bars = []
        for c in range(per):
            cols = pl.ds(c * width, width)
            old = x[:, cols]
            new = jnp.minimum(jnp.maximum(old - step_primal * acc[c], 0.0), upper[:, cols])
            bars.append((2.0 * new - old).astype(jnp.bfloat16))
            x[:, cols] = new
        for j in (0, 4, 1, 3, 2):
            mark = marks(j)
            picked = [bars[0], bars[per - 1]]
            for s in range(2, per):
                chosen = bars[0].astype(jnp.float32)
                for c in range(1, per):
                    chosen = jnp.where(mark[s] == c, bars[c].astype(jnp.float32), chosen)
                picked.append(chosen.astype(jnp.bfloat16))
            picked = jnp.concatenate(picked, axis=1)
            if it == 0:
                terms = lax.dot_general(
                    picked, blocks_of(j), (((1,), (1,)), ((), ())), preferred_element_type=jnp.float32
                )
            else:
                terms = jnp.dot(picked, kt[j], preferred_element_type=jnp.float32)
            if j == REACH:
                zown[...] = terms
            else:
                change = (terms if it == 0 else terms - zheld[j]).astype(jnp.bfloat16)
                zsend[it, j] = change
                if not last:
                    zheld[j] = change.astype(jnp.float32) if it == 0 else zheld[j] + change.astype(jnp.float32)
                remote(zsend.at[it, j], zin.at[it, 2 * REACH - j], z_sends.at[it, j], z_recvs.at[it, 2 * REACH - j], j - REACH).start()
        if it == 0:
            for j in range(SPAN):
                for s in range(per):
                    kt[j, pl.ds(s * width, width), :] = kb[j, s].T
        others = jnp.zeros((scen, width), jnp.float32) if it == 0 else zsum[...]
        for j in (1, 3, 0, 4):
            remote(zsend.at[it, j], zin.at[it, j], z_sends.at[it, j], z_recvs.at[it, j], REACH - j).wait_recv()
            others = others + zin[it, j].astype(jnp.float32)
        if not last:
            zsum[...] = others
        new_y = jnp.maximum(y[...] + step_dual * (zown[...] + others - bound[...]), 0.0)
        y[...] = new_y
        if not last:
            ysend[it + 1, pl.ds(0, scen), :] = new_y.astype(jnp.bfloat16)
            for o in OFFSETS:
                remote(
                    ysend.at[it + 1, pl.ds(0, scen)],
                    yin.at[it, REACH - o],
                    y_sends.at[it + 1, REACH - o],
                    y_recvs.at[it + 1, REACH - o],
                    o,
                ).start()
    for o in OFFSETS:
        heads[o].wait_send()
        blocks_out[o].wait_send()
        for it in range(1, ITERS):
            remote(ysend.at[it, pl.ds(0, scen)], yin.at[it - 1, REACH - o], y_sends.at[it, REACH - o], y_recvs.at[it, REACH - o], o).wait_send()
        for it in range(ITERS):
            j = o + REACH
            remote(zsend.at[it, j], zin.at[it, j], z_sends.at[it, j], z_recvs.at[it, j], o).wait_send()


def finish(x_in, y_in, x_out, y_out, sems):
    copies = [
        pltpu.make_async_copy(x_in, x_out, sems.at[0]),
        pltpu.make_async_copy(y_in, y_out, sems.at[1]),
    ]
    for copy in copies:
        copy.start()
    for copy in copies:
        copy.wait()


def per_device(n_dev, paired, blocks, col_index, cost, upper, capacity, disrupted, x_start, y_start):
    slots, width = blocks.shape[1], blocks.shape[3]
    per = slots // SPAN
    scen, ncols = x_start.shape
    rows_head = scen + 32
    f32, bf16 = jnp.float32, jnp.bfloat16
    anyspace = pl.BlockSpec(memory_space=pl.ANY)
    dma = pltpu.SemaphoreType.DMA
    shapes = (
        jax.ShapeDtypeStruct(x_start.shape, f32),
        jax.ShapeDtypeStruct(y_start.shape, f32),
    )
    ends = pl.pallas_call(
        functools.partial(kernel, n_dev, paired),
        out_shape=shapes,
        in_specs=[anyspace] * 8,
        out_specs=(pl.BlockSpec(memory_space=pltpu.VMEM),) * 2,
        scratch_shapes=[
            pltpu.SMEM(col_index.shape, jnp.int32),
            pltpu.VMEM((SPAN, per, width, width), bf16),
            pltpu.VMEM((SPAN, per * width, width), bf16),
            pltpu.VMEM((rows_head, width), f32),
            pltpu.VMEM((SPAN, rows_head, width), bf16),
            pltpu.VMEM((ITERS, rows_head, width), bf16),
            pltpu.VMEM((ITERS - 1, SPAN, scen, width), bf16),
            pltpu.VMEM((ITERS, SPAN, scen, width), bf16),
            pltpu.VMEM((ITERS, SPAN, scen, width), bf16),
            pltpu.VMEM((scen, width), f32),
            pltpu.VMEM((SPAN, scen, width), f32),
            pltpu.VMEM((scen, width), f32),
            pltpu.VMEM((1, ncols), f32),
            pltpu.VMEM((1, ncols), f32),
            pltpu.VMEM((1, width), f32),
            pltpu.VMEM((scen, width), jnp.int32),
            pltpu.VMEM((scen, width), f32),
            dma((8,)),
            dma((SPAN,)),
            dma((SPAN,)),
            dma((ITERS, SPAN)),
            dma((ITERS, SPAN)),
            dma((ITERS, SPAN)),
            dma((ITERS, SPAN)),
            pltpu.SemaphoreType.REGULAR,
        ],
        compiler_params=pltpu.CompilerParams(
            collective_id=0, has_side_effects=True, vmem_limit_bytes=32 * 1024 * 1024
        ),
    )(
        *(
            pltpu.with_memory_space_constraint(operand, pltpu.HBM)
            for operand in (
                col_index,
                blocks,
                cost.reshape(1, -1),
                upper.reshape(1, -1),
                capacity.reshape(1, -1),
                disrupted,
                x_start,
                y_start,
            )
        )
    )
    return pl.pallas_call(
        finish,
        out_shape=shapes,
        in_specs=[anyspace] * 2,
        out_specs=(anyspace, anyspace),
        scratch_shapes=[dma((2,))],
    )(*(pltpu.with_memory_space_constraint(end, pltpu.VMEM) for end in ends))


def solution(mesh):
    placed = (
        P(("scen", "blk"), None, None, None),
        P(("scen", "blk"), None),
        P(("scen", "blk")),
        P(("scen", "blk")),
        P(("scen", "blk")),
        P("scen", "blk"),
        P("scen", "blk"),
        P("scen", "blk"),
    )
    return jax.shard_map(
        functools.partial(per_device, mesh.shape["blk"], mesh.shape["scen"] % 2 == 0),
        mesh=mesh,
        in_specs=placed,
        out_specs=(P("scen", "blk"), P("scen", "blk")),
        check_vma=False,
    )
```

```python
import functools

import jax
import jax.numpy as jnp
from jax import lax
from jax.experimental import pallas as pl
from jax.experimental.pallas import tpu as pltpu
from jax.sharding import PartitionSpec as P

MESH = pl.DeviceIdType.MESH

REACH = 2
ITERS = 4
SPAN = 2 * REACH + 1
OFFSETS = (-2, 2, -1, 1)

step_primal = 0.4
step_dual = 0.4


def kernel(
    n_dev,
    paired,
    idx_hbm,
    blocks_ref,
    cost_ref,
    upper_ref,
    cap_ref,
    dis_ref,
    xs_ref,
    ys_ref,
    x,
    y,
    idx_ref,
    kb,
    kt,
    head,
    head_in,
    ysend,
    yin,
    zsend,
    zin,
    zown,
    zheld,
    zsum,
    cost,
    upper,
    cap,
    dis,
    bound,
    load_sem,
    kb_send,
    kb_recv,
    y_sends,
    y_recvs,
    z_sends,
    z_recvs,
    turn,
):
    per = kb.shape[1]
    width = kb.shape[2]
    scen = x.shape[0]
    me = lax.axis_index("blk")

    def remote(source, target, send, recv, offset):
        return pltpu.make_async_remote_copy(
            src_ref=source,
            dst_ref=target,
            send_sem=send,
            recv_sem=recv,
            device_id={"blk": lax.rem(me + offset + n_dev, n_dev)},
            device_id_type=MESH,
        )

    barrier = pltpu.get_barrier_semaphore()
    for offset in OFFSETS:
        pl.semaphore_signal(
            barrier, inc=1, device_id={"blk": lax.rem(me + offset + n_dev, n_dev)}, device_id_type=MESH
        )
    if paired:
        group = lax.axis_index("scen")
        second = lax.rem(group, 2)
        twin = {"scen": group + 1 - 2 * second}
        pl.semaphore_signal(barrier, inc=1, device_id=twin, device_id_type=MESH)

    loads = [
        pltpu.make_async_copy(ys_ref, y, load_sem.at[0]),
        pltpu.make_async_copy(idx_hbm, idx_ref, load_sem.at[7]),
        pltpu.make_async_copy(blocks_ref.at[0, pl.ds(REACH * per, per)], kb.at[REACH], load_sem.at[1]),
        pltpu.make_async_copy(xs_ref, x, load_sem.at[2]),
        pltpu.make_async_copy(cost_ref, cost, load_sem.at[3]),
        pltpu.make_async_copy(upper_ref, upper, load_sem.at[4]),
        pltpu.make_async_copy(cap_ref, cap, load_sem.at[5]),
        pltpu.make_async_copy(dis_ref, dis, load_sem.at[6]),
    ]
    for load in loads:
        load.start()
    blocks_out = {
        o: remote(
            blocks_ref.at[0, pl.ds((REACH + o) * per, per)],
            kb.at[REACH - o],
            kb_send.at[REACH - o],
            kb_recv.at[REACH - o],
            o,
        )
        for o in OFFSETS
    }

    def send_blocks(offsets):
        for o in offsets:
            blocks_out[o].start()

    pl.semaphore_wait(barrier, 2 * REACH + (1 if paired else 0))
    if paired:
        pl.when(second == 0)(lambda: send_blocks((-1, 1)))
    else:
        send_blocks((-1, 1))

    loads[0].wait()
    loads[1].wait()
    head[pl.ds(scen, head.shape[0] - scen), :] = jnp.zeros((head.shape[0] - scen, width), jnp.float32)
    for slot in range(SPAN * per):
        head[pl.ds(scen + slot, 1), :] = jnp.full((1, width), lax.rem(idx_ref[0, slot], per), jnp.float32)
    head[pl.ds(0, scen), :] = y[...].astype(jnp.bfloat16).astype(jnp.float32)
    ysend[0] = head[...].astype(jnp.bfloat16)
    heads = {o: remote(ysend.at[0], head_in.at[REACH - o], y_sends.at[0, REACH - o], y_recvs.at[0, REACH - o], o) for o in OFFSETS}
    for o in OFFSETS:
        heads[o].start()
    if paired:
        pl.when(second == 0)(lambda: send_blocks((-2, 2)))

        @pl.when(second == 1)
        def _():
            pl.semaphore_wait(turn, 1)
            send_blocks((-1, 1, -2, 2))
    else:
        send_blocks((-2, 2))

    for load in loads[2:]:
        load.wait()
    bound[...] = cap[...] * jnp.where(dis[...] == 1, 0.25, 1.0)

    def blocks_of(j):
        return jnp.concatenate([kb[j, s] for s in range(per)], axis=1)

    def marks(j):
        base = scen + (SPAN - 1 - j) * per
        source = head if j == REACH else head_in.at[j]
        rows = source[pl.ds(base, per), :].astype(jnp.float32)
        return [jnp.broadcast_to(rows[s : s + 1, :], (scen, width)) for s in range(per)]

    for it in range(ITERS):
        last = it == ITERS - 1
        acc = [jnp.broadcast_to(cost[:, pl.ds(c * width, width)], (scen, width)) for c in range(per)]
        for near in ((REACH,), (1, 3), (0, 4)):
            for j in near:
                if j != REACH and it == 0:
                    heads[REACH - j].wait_recv()
                    blocks_out[REACH - j].wait_recv()
                elif j != REACH:
                    remote(ysend.at[it, pl.ds(0, scen)], yin.at[it - 1, j], y_sends.at[it, j], y_recvs.at[it, j], REACH - j).wait_recv()
            if paired and it == 0 and near == (1, 3):

                @pl.when(second == 0)
                def _():
                    pl.semaphore_signal(turn, inc=1, device_id=twin, device_id_type=MESH)

            for j in near:
                if j == REACH:
                    low = ysend[it, pl.ds(0, scen), :]
                elif it == 0:
                    low = head_in[j, pl.ds(0, scen), :]
                else:
                    low = yin[it - 1, j]
                terms = jnp.dot(low, blocks_of(j), preferred_element_type=jnp.float32)
                acc[0] = acc[0] + terms[:, :width]
                acc[per - 1] = acc[per - 1] + terms[:, width : 2 * width]
                mark = marks(j)
                for s in range(2, per):
                    part = terms[:, s * width : (s + 1) * width]
                    for c in range(per):
                        acc[c] = acc[c] + jnp.where(mark[s] == c, part, 0.0)
        bars = []
        for c in range(per):
            cols = pl.ds(c * width, width)
            old = x[:, cols]
            new = jnp.minimum(jnp.maximum(old - step_primal * acc[c], 0.0), upper[:, cols])
            bars.append((2.0 * new - old).astype(jnp.bfloat16))
            x[:, cols] = new
        for far in ((0, 4, 1, 3), (REACH,)):
            terms = {}
            for j in far:
                mark = marks(j)
                picked = [bars[0], bars[per - 1]]
                for s in range(2, per):
                    chosen = bars[0].astype(jnp.float32)
                    for c in range(1, per):
                        chosen = jnp.where(mark[s] == c, bars[c].astype(jnp.float32), chosen)
                    picked.append(chosen.astype(jnp.bfloat16))
                picked = jnp.concatenate(picked, axis=1)
                if it == 0:
                    terms[j] = lax.dot_general(
                        picked, blocks_of(j), (((1,), (1,)), ((), ())), preferred_element_type=jnp.float32
                    )
                else:
                    terms[j] = jnp.dot(picked, kt[j], preferred_element_type=jnp.float32)
            if far == (REACH,):
                zown[...] = terms[REACH]
                continue
            changes = {}
            for j in far:
                changes[j] = (terms[j] if it == 0 else terms[j] - zheld[j]).astype(jnp.bfloat16)
                zsend[it, j] = changes[j]
            for j in far:
                remote(zsend.at[it, j], zin.at[it, 2 * REACH - j], z_sends.at[it, j], z_recvs.at[it, 2 * REACH - j], j - REACH).start()
            if not last:
                for j in far:
                    zheld[j] = changes[j].astype(jnp.float32) if it == 0 else zheld[j] + changes[j].astype(jnp.float32)
        if it == 0:
            for j in range(SPAN):
                for s in range(per):
                    kt[j, pl.ds(s * width, width), :] = kb[j, s].T
        others = jnp.zeros((scen, width), jnp.float32) if it == 0 else zsum[...]
        for j in (1, 3, 0, 4):
            remote(zsend.at[it, j], zin.at[it, j], z_sends.at[it, j], z_recvs.at[it, j], REACH - j).wait_recv()
        for j in (1, 3, 0, 4):
            others = others + zin[it, j].astype(jnp.float32)
        new_y = jnp.maximum(y[...] + step_dual * (zown[...] + others - bound[...]), 0.0)
        if not last:
            ysend[it + 1, pl.ds(0, scen), :] = new_y.astype(jnp.bfloat16)
            for o in OFFSETS:
                remote(
                    ysend.at[it + 1, pl.ds(0, scen)],
                    yin.at[it, REACH - o],
                    y_sends.at[it + 1, REACH - o],
                    y_recvs.at[it + 1, REACH - o],
                    o,
                ).start()
            zsum[...] = others
        y[...] = new_y
    for o in OFFSETS:
        heads[o].wait_send()
        blocks_out[o].wait_send()
        for it in range(1, ITERS):
            remote(ysend.at[it, pl.ds(0, scen)], yin.at[it - 1, REACH - o], y_sends.at[it, REACH - o], y_recvs.at[it, REACH - o], o).wait_send()
        for it in range(ITERS):
            j = o + REACH
            remote(zsend.at[it, j], zin.at[it, j], z_sends.at[it, j], z_recvs.at[it, j], o).wait_send()


def finish(x_in, y_in, x_out, y_out, sems):
    copies = [
        pltpu.make_async_copy(x_in, x_out, sems.at[0]),
        pltpu.make_async_copy(y_in, y_out, sems.at[1]),
    ]
    for copy in copies:
        copy.start()
    for copy in copies:
        copy.wait()


def per_device(n_dev, paired, blocks, col_index, cost, upper, capacity, disrupted, x_start, y_start):
    slots, width = blocks.shape[1], blocks.shape[3]
    per = slots // SPAN
    scen, ncols = x_start.shape
    rows_head = scen + 32
    f32, bf16 = jnp.float32, jnp.bfloat16
    anyspace = pl.BlockSpec(memory_space=pl.ANY)
    dma = pltpu.SemaphoreType.DMA
    shapes = (
        jax.ShapeDtypeStruct(x_start.shape, f32),
        jax.ShapeDtypeStruct(y_start.shape, f32),
    )
    ends = pl.pallas_call(
        functools.partial(kernel, n_dev, paired),
        out_shape=shapes,
        in_specs=[anyspace] * 8,
        out_specs=(pl.BlockSpec(memory_space=pltpu.VMEM),) * 2,
        scratch_shapes=[
            pltpu.SMEM(col_index.shape, jnp.int32),
            pltpu.VMEM((SPAN, per, width, width), bf16),
            pltpu.VMEM((SPAN, per * width, width), bf16),
            pltpu.VMEM((rows_head, width), f32),
            pltpu.VMEM((SPAN, rows_head, width), bf16),
            pltpu.VMEM((ITERS, rows_head, width), bf16),
            pltpu.VMEM((ITERS - 1, SPAN, scen, width), bf16),
            pltpu.VMEM((ITERS, SPAN, scen, width), bf16),
            pltpu.VMEM((ITERS, SPAN, scen, width), bf16),
            pltpu.VMEM((scen, width), f32),
            pltpu.VMEM((SPAN, scen, width), f32),
            pltpu.VMEM((scen, width), f32),
            pltpu.VMEM((1, ncols), f32),
            pltpu.VMEM((1, ncols), f32),
            pltpu.VMEM((1, width), f32),
            pltpu.VMEM((scen, width), jnp.int32),
            pltpu.VMEM((scen, width), f32),
            dma((8,)),
            dma((SPAN,)),
            dma((SPAN,)),
            dma((ITERS, SPAN)),
            dma((ITERS, SPAN)),
            dma((ITERS, SPAN)),
            dma((ITERS, SPAN)),
            pltpu.SemaphoreType.REGULAR,
        ],
        compiler_params=pltpu.CompilerParams(
            collective_id=0, has_side_effects=True, vmem_limit_bytes=32 * 1024 * 1024
        ),
    )(
        *(
            pltpu.with_memory_space_constraint(operand, pltpu.HBM)
            for operand in (
                col_index,
                blocks,
                cost.reshape(1, -1),
                upper.reshape(1, -1),
                capacity.reshape(1, -1),
                disrupted,
                x_start,
                y_start,
            )
        )
    )
    return pl.pallas_call(
        finish,
        out_shape=shapes,
        in_specs=[anyspace] * 2,
        out_specs=(anyspace, anyspace),
        scratch_shapes=[dma((2,))],
    )(*(pltpu.with_memory_space_constraint(end, pltpu.VMEM) for end in ends))


def solution(mesh):
    placed = (
        P(("scen", "blk"), None, None, None),
        P(("scen", "blk"), None),
        P(("scen", "blk")),
        P(("scen", "blk")),
        P(("scen", "blk")),
        P("scen", "blk"),
        P("scen", "blk"),
        P("scen", "blk"),
    )
    return jax.shard_map(
        functools.partial(per_device, mesh.shape["blk"], mesh.shape["scen"] % 2 == 0),
        mesh=mesh,
        in_specs=placed,
        out_specs=(P("scen", "blk"), P("scen", "blk")),
        check_vma=False,
    )
```
